32 devices in a mesh: dp: 16 (over z, x, core), head: 2 (over y).
Axes of the slice: x: 2, y: 2, z: 4, core: 2. Of those that a mesh axis runs over, the one named last changes fastest.
Arguments:
- queries: bfloat16 [4096, 8192], P('dp', 'head'), may hold values from -6 to 6
- keys: bfloat16 [4096, 1024], P('dp', 'head'), may hold values from -6 to 6
- values: bfloat16 [4096, 1024], P('dp', 'head'), may hold values from -6 to 6
- output_grad: bfloat16 [4096, 4096], P('dp', 'head'), may hold values from -6 to 6
- out_weight: bfloat16 [8192, 4096], P(('head', 'dp')), may hold values from -0.0625 to 0.0625
- lengths: int32 [16], replicated, may hold values from 1 to 512, 4096 in all
Outputs:
- layer_out: bfloat16 [4096, 4096], P('dp', 'head')
- query_grad: bfloat16 [4096, 8192], P('dp', 'head')
- key_grad: bfloat16 [4096, 1024], P('dp', 'head')
- value_grad: bfloat16 [4096, 1024], P('dp', 'head')
The draws below stay inside these ranges and needn't reach their ends.
Inputs may be any that keep to these rules, and one draw needn't show every extreme that they name: Each of the 16 lengths is at least 1 and at most 512, they sum to 4096, and one equals 512.
All inputs are finite; a program needn't handle non-finite values.
Results may differ from the reference program's by a relative error of at most 0.028.
Values may be sent and summed in bfloat16 or wider, within the bound.
A program may use at most 128 MiB of HBM per device.

```python
import math
import jax
import jax.numpy as jnp
import numpy as np
from jax import lax

HEADS = 64
KV_HEADS = 8
HD = 128
DW = 4096
TOK_DEV = 256
SPAN = 2
LENGTH = 4096
MOST = 512
DOCS = 16
N_DP = 16


def draw_queries(key, part):
    base = jnp.clip(jax.random.normal(jax.random.fold_in(key, 1), (LENGTH, HEADS * HD)), -4.0, 4.0)
    return base.astype(jnp.bfloat16)


def draw_keys(key, part):
    base = jnp.clip(jax.random.normal(jax.random.fold_in(key, 2), (LENGTH, KV_HEADS * HD)), -4.0, 4.0)
    return base.astype(jnp.bfloat16)


def block_levels(key, shape, pieces, low, top_value):
    factor_of = 1.0
    for position, blocks in pieces:
        steps = jax.random.uniform(jax.random.fold_in(jax.random.fold_in(key, 6), position), (blocks,), jnp.float32, low / len(pieces), top_value / len(pieces))
        factor_of = factor_of * jnp.repeat(jnp.exp(steps), shape[position] // blocks).reshape((-1,) + (1,) * (len(shape) - 1 - position))
    return factor_of


def split_up(count, total, limit, lean):
    loads = [(1 << 20) // math.isqrt(grade ** lean) + 1 for grade in range(2, count + 1)]
    surplus, holding = total - limit - (count - 1), [1] * (count - 1)
    while surplus > 0:
        candidates = [i for i in range(count - 1) if holding[i] < limit]
        whole, remaining = sum([loads[i] for i in candidates]), surplus
        for i in candidates:
            more = min(limit - holding[i], max(1, remaining * loads[i] // whole), surplus)
            holding[i] = holding[i] + more
            surplus = surplus - more
    return np.array([limit] + holding)


def ragged_sizes(key, number_of, total, limit, skew):
    if number_of == 2:
        one = jax.random.randint(key, (), max(1, total - limit), min(limit, total - 1) + 1)
        return jnp.stack([one, total - one])
    tallies = jnp.asarray(split_up(number_of, total, limit, skew), jnp.int32)
    twos = (number_of - 1) // 2
    giver, receiver = tallies[1:1 + 2 * twos:2], tallies[2:2 + 2 * twos:2]
    margin = jnp.minimum(giver - 1, limit - receiver)
    moved = jax.random.randint(jax.random.fold_in(key, 1), (twos,), 0, 1 << 20) % (margin + 1)
    tallies = tallies.at[1:1 + 2 * twos:2].set(giver - moved).at[2:2 + 2 * twos:2].set(receiver + moved)
    return tallies[jax.random.permutation(jax.random.fold_in(key, 2), number_of)]


def normal_values(key, extent, width, most, shards=(), held_as=jnp.bfloat16):
    array = jax.random.normal(key, extent, jnp.float32) * width
    if len(shards) > 0:
        array = block_levels(key, extent, shards, -0.22, 0.18) * array
    return jnp.clip(array, min=-most, max=most).astype(held_as)


def setup_inputs(seed: int = 0) -> dict:
    splits = jax.random.split(jax.random.key(seed), 7)
    queries = draw_queries(jax.random.fold_in(splits[6], 71), 0)
    keys = draw_keys(jax.random.fold_in(splits[6], 71), 0)
    values = normal_values(splits[2], (LENGTH, KV_HEADS * HD), 1.0, 6.0, ((0, 16), (1, 2)))
    output_grad = normal_values(splits[3], (LENGTH, DW), 1.0, 6.0, ((0, 16), (1, 2)))
    out_weight = normal_values(splits[4], (HEADS * HD, DW), (HEADS * HD) ** -0.5, 0.0625, ((0, 32),))
    lengths = ragged_sizes(splits[5], DOCS, LENGTH, MOST, 2).astype(jnp.int32)
    return {"queries": queries, "keys": keys, "values": values, "output_grad": output_grad, "out_weight": out_weight, "lengths": lengths}


masked_score = -1e+30

def doc_start(lengths, positions):
    lengths = lengths.astype(jnp.int32)
    doc_ends = jnp.cumsum(lengths).astype(jnp.int32)
    closed = doc_ends[None, :] <= positions[:, None]
    return lax.optimization_barrier(jnp.sum(jnp.where(closed, lengths[None, :], 0), axis=1)).astype(jnp.int32)

def attend(queries, key_rows, value_rows, d_attended, visible, head_dim):
    row_count = queries.shape[0]
    kv_heads = key_rows.shape[1] // head_dim
    group_ratio = queries.shape[1] // key_rows.shape[1]
    scaling = 1.0 / math.sqrt(head_dim)
    grouped = queries.reshape(row_count, kv_heads, group_ratio, head_dim).astype(jnp.float32)
    keyed = key_rows.reshape(-1, kv_heads, head_dim).astype(jnp.float32)
    valued = value_rows.reshape(-1, kv_heads, head_dim).astype(jnp.float32)
    upstream = d_attended.reshape(row_count, kv_heads, group_ratio, head_dim).astype(jnp.float32)
    scores = jnp.einsum('tgrd,ngd->grtn', grouped, keyed) * scaling
    scores = jnp.where(visible[None, None], scores, masked_score)
    maximum = lax.optimization_barrier(jnp.max(scores, axis=-1, keepdims=True))
    weights = jnp.exp(scores - maximum)
    shares = weights / lax.optimization_barrier(jnp.sum(weights, axis=-1, keepdims=True))
    shares_low = lax.optimization_barrier(shares.astype(jnp.bfloat16)).astype(jnp.float32)
    attended = lax.optimization_barrier(jnp.einsum('grtn,ngd->tgrd', shares_low, valued).astype(jnp.bfloat16))
    attended_wide = attended.astype(jnp.float32)
    row_dots = lax.optimization_barrier(jnp.sum(upstream * attended_wide, axis=-1))
    d_shares = jnp.einsum('tgrd,ngd->grtn', upstream, valued)
    dscore = shares * (d_shares - jnp.transpose(row_dots, (1, 2, 0))[..., None]) * scaling
    dscore = lax.optimization_barrier(dscore.astype(jnp.bfloat16)).astype(jnp.float32)
    query_grad = jnp.einsum('grtn,ngd->tgrd', dscore, keyed).astype(jnp.bfloat16)
    key_part = jnp.einsum('grtn,tgrd->ngd', dscore, grouped)
    value_part = jnp.einsum('grtn,tgrd->ngd', shares_low, upstream)
    return (attended.reshape(row_count, -1), query_grad.reshape(row_count, -1), key_part.reshape(-1, kv_heads * head_dim), value_part.reshape(-1, kv_heads * head_dim))

def reference(queries, keys, values, output_grad, out_weight, lengths):
    block_rows = TOK_DEV
    window_rows = (SPAN + 1) * block_rows
    padding = SPAN * block_rows
    kv_width = keys.shape[1]
    d_attended = jnp.dot(output_grad, out_weight.T, preferred_element_type=jnp.float32).astype(jnp.bfloat16)
    padded_keys = jnp.concatenate([jnp.zeros((padding, kv_width), keys.dtype), keys], axis=0)
    padded_values = jnp.concatenate([jnp.zeros((padding, kv_width), values.dtype), values], axis=0)

    def one_block(running, block_index):
        key_acc, value_acc = running
        first_row = (block_index * block_rows).astype(jnp.int32)
        query_block = lax.dynamic_slice_in_dim(queries, first_row, block_rows, 0)
        grad_block = lax.dynamic_slice_in_dim(d_attended, first_row, block_rows, 0)
        key_block = lax.dynamic_slice_in_dim(padded_keys, first_row, window_rows, 0)
        value_block = lax.dynamic_slice_in_dim(padded_values, first_row, window_rows, 0)
        positions = first_row + jnp.arange(block_rows, dtype=jnp.int32)
        starts = doc_start(lengths, positions)
        key_positions = first_row - padding + jnp.arange(window_rows, dtype=jnp.int32)
        visible = (key_positions[None, :] >= starts[:, None]) & (key_positions[None, :] <= positions[:, None])
        attended, query_grad, key_part, value_part = attend(query_block, key_block, value_block, grad_block, visible, HD)
        key_acc = lax.dynamic_update_slice_in_dim(key_acc, lax.dynamic_slice_in_dim(key_acc, first_row, window_rows, 0) + key_part, first_row, 0)
        value_acc = lax.dynamic_update_slice_in_dim(value_acc, lax.dynamic_slice_in_dim(value_acc, first_row, window_rows, 0) + value_part, first_row, 0)
        return ((key_acc, value_acc), (attended, query_grad))
    zeroed = jnp.zeros((N_DP * block_rows + padding, kv_width), jnp.float32)
    (key_acc, value_acc), (attended_blocks, query_blocks) = lax.scan(one_block, (zeroed, zeroed), jnp.arange(N_DP, dtype=jnp.int32))
    attended_all = attended_blocks.reshape(-1, attended_blocks.shape[-1])
    layer_out = jnp.dot(attended_all, out_weight, preferred_element_type=jnp.float32).astype(jnp.bfloat16)
    query_grad = query_blocks.reshape(-1, query_blocks.shape[-1])
    return (layer_out, query_grad, key_acc[padding:].astype(jnp.bfloat16), value_acc[padding:].astype(jnp.bfloat16))
```

```python
import functools
import math

import jax
import jax.numpy as jnp
from jax import lax
from jax.experimental import pallas as pl
from jax.sharding import PartitionSpec as P

HD = 128
SPAN = 2

masked_score = -1e30


def passed_along(block, axis, distance):
    devices = range(lax.axis_size(axis))
    route = [(i - distance, i) for i in devices if i - distance in devices]
    return lax.ppermute(block, axis, route)


def swapped(block, axis):
    return lax.ppermute(block, axis, [(0, 1), (1, 0)])


def doc_start(lengths, positions):
    doc_ends = jnp.cumsum(lengths)
    closed = doc_ends[None, :] <= positions[:, None]
    return jnp.sum(jnp.where(closed, lengths[None, :], 0), axis=1)


def mm(a, b, contract):
    return lax.dot_general(a, b, ((contract[:1], contract[1:]), ((), ())), preferred_element_type=jnp.float32)


def forward_kernel(chunks, ratio, starts_ref, q_ref, kv_ref, *outs):
    att_refs, shares_ref = outs[:chunks], outs[chunks]
    rows = q_ref.shape[0]
    window = kv_ref.shape[1]
    keys = kv_ref[0]
    values_t = kv_ref[1].T
    key_pos = lax.broadcasted_iota(jnp.int32, (window, rows), 0)
    query_pos = lax.broadcasted_iota(jnp.int32, (window, rows), 1) + (window - rows)
    visible = (key_pos >= starts_ref[...]) & (key_pos <= query_pos)
    scaling = 1.0 / math.sqrt(HD)
    for h in range(ratio):
        c, j = h % chunks, h // chunks
        scores = mm(keys, q_ref[:, h * HD : (h + 1) * HD], (1, 1)) * scaling
        scores = jnp.where(visible, scores, masked_score)
        weights = jnp.exp(scores - jnp.max(scores, axis=0, keepdims=True))
        shares = (weights * (1.0 / jnp.sum(weights, axis=0, keepdims=True))).astype(jnp.bfloat16)
        shares_ref[c, 0, j] = shares
        attended = mm(values_t, shares, (1, 0))
        att_refs[c][:, j * HD : (j + 1) * HD] = attended.T.astype(jnp.bfloat16)


def attend_forward(starts, queries, kv, chunks):
    rows, heads = queries.shape[0], queries.shape[1] // HD
    window, groups = kv.shape[1], kv.shape[2] // HD
    ratio = heads // groups
    per = ratio // chunks
    return pl.pallas_call(
        functools.partial(forward_kernel, chunks, ratio),
        grid=(groups,),
        in_specs=[
            pl.BlockSpec((1, rows), lambda g: (0, 0)),
            pl.BlockSpec((rows, ratio * HD), lambda g: (0, g)),
            pl.BlockSpec((2, window, HD), lambda g: (0, 0, g)),
        ],
        out_specs=[pl.BlockSpec((rows, per * HD), lambda g: (0, g))] * chunks
        + [pl.BlockSpec((chunks, 1, per, window, rows), lambda g: (0, g, 0, 0, 0))],
        out_shape=[jax.ShapeDtypeStruct((rows, heads // chunks * HD), jnp.bfloat16)] * chunks
        + [jax.ShapeDtypeStruct((chunks, groups, per, window, rows), jnp.bfloat16)],
        cost_estimate=pl.CostEstimate(
            flops=8 * heads * rows * window * HD, bytes_accessed=2 * heads * rows * window, transcendentals=heads * rows * window
        ),
        name="attend_forward",
    )(starts, queries, kv)


def backward_kernel(c, chunks, ratio, *refs):
    per = ratio // chunks
    last = c == chunks - 1
    q_ref, kv_ref, shares_ref, da_ref, att_ref = refs[:5]
    earlier = refs[5 : 5 + c + (c > 0)]
    outs = refs[5 + len(earlier) :]
    rows = q_ref.shape[0]
    window = kv_ref.shape[1]
    keys_t = kv_ref[0].T
    values = kv_ref[1]
    scaling = 1.0 / math.sqrt(HD)
    dk = earlier[-1][0] if c > 0 else jnp.zeros((window, HD), jnp.float32)
    dv = earlier[-1][1] if c > 0 else jnp.zeros((window, HD), jnp.float32)
    for j in range(per):
        h = j * chunks + c
        da = da_ref[:, j * HD : (j + 1) * HD]
        att = att_ref[:, j * HD : (j + 1) * HD]
        shares = shares_ref[0, 0, j]
        row_dots = jnp.sum((da.astype(jnp.float32) * att.astype(jnp.float32)).T, axis=0, keepdims=True)
        d_shares = mm(values, da, (1, 1))
        dscore = (shares.astype(jnp.float32) * ((d_shares - row_dots) * scaling)).astype(jnp.bfloat16)
        dq = mm(keys_t, dscore, (1, 0)).T.astype(jnp.bfloat16)
        place = h if last else j
        outs[0][:, place * HD : (place + 1) * HD] = dq
        if last:
            for b in range(c):
                where = j * chunks + b
                outs[0][:, where * HD : (where + 1) * HD] = earlier[b][:, j * HD : (j + 1) * HD]
        dk = dk + mm(dscore, q_ref[:, h * HD : (h + 1) * HD], (1, 0))
        dv = dv + mm(shares, da, (1, 0))
    if last:
        for part, total in ((0, dk), (1, dv)):
            outs[1][part] = total[window - rows :]
            for offset in range(1, SPAN + 1):
                first = window - (offset + 1) * rows
                outs[1 + offset][part] = total[first : first + rows].astype(jnp.bfloat16)
    else:
        outs[1][0] = dk
        outs[1][1] = dv


def attend_backward(c, chunks, queries, kv, shares, d_attended, attended, earlier):
    rows, heads = queries.shape[0], queries.shape[1] // HD
    window, groups = kv.shape[1], kv.shape[2] // HD
    ratio = heads // groups
    per = ratio // chunks
    last = c == chunks - 1
    wide = pl.BlockSpec((rows, ratio * HD), lambda g: (0, g))
    narrow = pl.BlockSpec((rows, per * HD), lambda g: (0, g))
    pair = pl.BlockSpec((2, window, HD), lambda g: (0, 0, g))
    home = pl.BlockSpec((2, rows, HD), lambda g: (0, 0, g))
    if last:
        out_specs = [wide] + [home] * (SPAN + 1)
        out_shape = [
            jax.ShapeDtypeStruct(queries.shape, jnp.bfloat16),
            jax.ShapeDtypeStruct((2, rows, groups * HD), jnp.float32),
        ] + [jax.ShapeDtypeStruct((2, rows, groups * HD), jnp.bfloat16)] * SPAN
    else:
        out_specs = [narrow, pair]
        out_shape = [
            jax.ShapeDtypeStruct((rows, heads // chunks * HD), jnp.bfloat16),
            jax.ShapeDtypeStruct(kv.shape, jnp.float32),
        ]
    return pl.pallas_call(
        functools.partial(backward_kernel, c, chunks, ratio),
        grid=(groups,),
        in_specs=[
            wide,
            pair,
            pl.BlockSpec((1, 1, per, window, rows), lambda g: (c, g, 0, 0, 0)),
            narrow,
            narrow,
        ]
        + ([narrow] * c + [pair] if c > 0 else []),
        out_specs=out_specs,
        out_shape=out_shape,
        cost_estimate=pl.CostEstimate(
            flops=16 * heads // chunks * rows * window * HD,
            bytes_accessed=2 * heads // chunks * rows * window,
            transcendentals=0,
        ),
    )(queries, kv, shares, d_attended, attended, *earlier)


def whole_step(queries, keys, values, output_grad, out_weight, lengths):
    block_rows = queries.shape[0]
    device = lax.axis_index("dp")
    side = lax.axis_index("head")
    two_sided = lax.axis_size("head") == 2
    own_width = output_grad.shape[1]
    ratio = queries.shape[1] // keys.shape[1]
    chunks = out_weight.shape[0] // HD if out_weight.shape[0] % HD == 0 else 1
    if chunks == 0 or ratio % chunks:
        chunks = 1
    depth = out_weight.shape[0] // chunks

    weights = [
        lax.all_gather(out_weight[c * depth : (c + 1) * depth], "dp", axis=0, tiled=True)
        for c in range(chunks)
    ]
    couple = jnp.stack([keys, values])
    earlier = [passed_along(couple, "dp", offset) for offset in range(1, SPAN + 1)]
    kv = jnp.concatenate(earlier[::-1] + [couple], axis=1)
    if two_sided:
        other = swapped(output_grad, "head")
        upstream_all = jnp.where(
            side == 0,
            jnp.concatenate([output_grad, other], axis=1),
            jnp.concatenate([other, output_grad], axis=1),
        )
    else:
        upstream_all = lax.all_gather(output_grad, "head", axis=1, tiled=True)

    positions = device * block_rows + jnp.arange(block_rows, dtype=jnp.int32)
    starts = doc_start(lengths, positions) - (device - SPAN) * block_rows
    *attended, shares = attend_forward(starts[None, :], queries, kv, chunks)

    projected = None
    query_parts, total = [], None
    for c in range(chunks):
        d_attended = mm(upstream_all, weights[c], (1, 1)).astype(jnp.bfloat16)
        part = mm(attended[c], weights[c], (1, 0))
        projected = part if projected is None else projected + part
        if c == chunks - 1:
            if two_sided:
                theirs = lax.dynamic_slice_in_dim(projected, (1 - side) * own_width, own_width, 1)
                ours = lax.dynamic_slice_in_dim(projected, side * own_width, own_width, 1)
            else:
                theirs, ours = projected, projected
            d_attended, theirs = lax.optimization_barrier((d_attended, theirs.astype(jnp.bfloat16)))
        passed = query_parts + [total] if c > 0 else []
        query_grad, *sums = attend_backward(
            c, chunks, queries, kv, shares, d_attended, attended[c], passed
        )
        if c < chunks - 1:
            query_parts.append(query_grad)
            total, projected, upstream_all, attended[c + 1] = lax.optimization_barrier(
                (sums[0], projected, upstream_all, attended[c + 1])
            )

    if two_sided:
        arrived = swapped(theirs, "head")
        layer_out = (ours + arrived.astype(jnp.float32)).astype(jnp.bfloat16)
    else:
        layer_out = lax.psum_scatter(theirs, "head", scatter_dimension=1, tiled=True)
    home = sums[0]
    for offset in range(1, SPAN + 1):
        home = home + passed_along(sums[offset], "dp", -offset).astype(jnp.float32)
    home = home.astype(jnp.bfloat16)
    return layer_out, query_grad, home[0], home[1]


def solution(mesh):
    return jax.shard_map(
        whole_step,
        mesh=mesh,
        in_specs=(
            P("dp", "head"),
            P("dp", "head"),
            P("dp", "head"),
            P("dp", "head"),
            P(("head", "dp"), None),
            P(),
        ),
        out_specs=(P("dp", "head"), P("dp", "head"), P("dp", "head"), P("dp", "head")),
        check_vma=False,
    )
```

```python
import functools
import math

import jax
import jax.numpy as jnp
from jax import lax
from jax.experimental import pallas as pl
from jax.sharding import PartitionSpec as P

HD = 128
SPAN = 2

masked_score = -1e30


def passed_along(block, axis, distance):
    devices = range(lax.axis_size(axis))
    route = [(i - distance, i) for i in devices if i - distance in devices]
    return lax.ppermute(block, axis, route)


def swapped(block, axis):
    return lax.ppermute(block, axis, [(0, 1), (1, 0)])


def doc_start(lengths, positions):
    doc_ends = jnp.cumsum(lengths)
    closed = doc_ends[None, :] <= positions[:, None]
    return jnp.sum(jnp.where(closed, lengths[None, :], 0), axis=1)


def mm(a, b, contract):
    return lax.dot_general(a, b, ((contract[:1], contract[1:]), ((), ())), preferred_element_type=jnp.float32)


def forward_kernel(chunks, ratio, starts_ref, q_ref, kv_ref, *outs):
    att_refs, shares_ref = outs[:chunks], outs[chunks]
    rows = q_ref.shape[0]
    window = kv_ref.shape[1]
    keys = kv_ref[0]
    values_t = kv_ref[1].T
    key_pos = lax.broadcasted_iota(jnp.int32, (window, rows), 0)
    query_pos = lax.broadcasted_iota(jnp.int32, (window, rows), 1) + (window - rows)
    visible = (key_pos >= starts_ref[...]) & (key_pos <= query_pos)
    scaling = 1.0 / math.sqrt(HD)
    for h in range(ratio):
        c, j = h % chunks, h // chunks
        scores = mm(keys, q_ref[:, h * HD : (h + 1) * HD], (1, 1)) * scaling
        scores = jnp.where(visible, scores, masked_score)
        weights = jnp.exp(scores - jnp.max(scores, axis=0, keepdims=True))
        shares = (weights * (1.0 / jnp.sum(weights, axis=0, keepdims=True))).astype(jnp.bfloat16)
        shares_ref[c, 0, j] = shares
        attended = mm(values_t, shares, (1, 0))
        att_refs[c][:, j * HD : (j + 1) * HD] = attended.T.astype(jnp.bfloat16)


def attend_forward(starts, queries, kv, chunks):
    rows, heads = queries.shape[0], queries.shape[1] // HD
    window, groups = kv.shape[1], kv.shape[2] // HD
    ratio = heads // groups
    per = ratio // chunks
    return pl.pallas_call(
        functools.partial(forward_kernel, chunks, ratio),
        grid=(groups,),
        in_specs=[
            pl.BlockSpec((1, rows), lambda g: (0, 0)),
            pl.BlockSpec((rows, ratio * HD), lambda g: (0, g)),
            pl.BlockSpec((2, window, HD), lambda g: (0, 0, g)),
        ],
        out_specs=[pl.BlockSpec((rows, per * HD), lambda g: (0, g))] * chunks
        + [pl.BlockSpec((chunks, 1, per, window, rows), lambda g: (0, g, 0, 0, 0))],
        out_shape=[jax.ShapeDtypeStruct((rows, heads // chunks * HD), jnp.bfloat16)] * chunks
        + [jax.ShapeDtypeStruct((chunks, groups, per, window, rows), jnp.bfloat16)],
        cost_estimate=pl.CostEstimate(
            flops=8 * heads * rows * window * HD, bytes_accessed=2 * heads * rows * window, transcendentals=heads * rows * window
        ),
        name="attend_forward",
    )(starts, queries, kv)


def backward_kernel(c, chunks, ratio, *refs):
    per = ratio // chunks
    last = c == chunks - 1
    q_ref, kv_ref, shares_ref, da_ref, att_ref = refs[:5]
    earlier = refs[5 : 5 + c + (c > 0)]
    outs = refs[5 + len(earlier) :]
    rows = q_ref.shape[0]
    window = kv_ref.shape[1]
    keys_t = kv_ref[0].T
    values = kv_ref[1]
    scaling = 1.0 / math.sqrt(HD)
    dk = earlier[-1][0] if c > 0 else jnp.zeros((window, HD), jnp.float32)
    dv = earlier[-1][1] if c > 0 else jnp.zeros((window, HD), jnp.float32)
    for j in range(per):
        h = j * chunks + c
        da = da_ref[:, j * HD : (j + 1) * HD]
        att = att_ref[:, j * HD : (j + 1) * HD]
        shares = shares_ref[0, 0, j]
        row_dots = jnp.sum((da.astype(jnp.float32) * att.astype(jnp.float32)).T, axis=0, keepdims=True)
        d_shares = mm(values, da, (1, 1))
        dscore = (shares.astype(jnp.float32) * ((d_shares - row_dots) * scaling)).astype(jnp.bfloat16)
        dq = mm(keys_t, dscore, (1, 0)).T.astype(jnp.bfloat16)
        place = h if last else j
        outs[0][:, place * HD : (place + 1) * HD] = dq
        if last:
            for b in range(c):
                where = j * chunks + b
                outs[0][:, where * HD : (where + 1) * HD] = earlier[b][:, j * HD : (j + 1) * HD]
        dk = dk + mm(dscore, q_ref[:, h * HD : (h + 1) * HD], (1, 0))
        dv = dv + mm(shares, da, (1, 0))
    if last:
        for part, total in ((0, dk), (1, dv)):
            outs[1][part] = total[window - rows :]
            for offset in range(1, SPAN + 1):
                first = window - (offset + 1) * rows
                outs[1 + offset][part] = total[first : first + rows].astype(jnp.bfloat16)
    else:
        outs[1][0] = dk
        outs[1][1] = dv


def attend_backward(c, chunks, queries, kv, shares, d_attended, attended, earlier):
    rows, heads = queries.shape[0], queries.shape[1] // HD
    window, groups = kv.shape[1], kv.shape[2] // HD
    ratio = heads // groups
    per = ratio // chunks
    last = c == chunks - 1
    wide = pl.BlockSpec((rows, ratio * HD), lambda g: (0, g))
    narrow = pl.BlockSpec((rows, per * HD), lambda g: (0, g))
    pair = pl.BlockSpec((2, window, HD), lambda g: (0, 0, g))
    home = pl.BlockSpec((2, rows, HD), lambda g: (0, 0, g))
    if last:
        out_specs = [wide] + [home] * (SPAN + 1)
        out_shape = [
            jax.ShapeDtypeStruct(queries.shape, jnp.bfloat16),
            jax.ShapeDtypeStruct((2, rows, groups * HD), jnp.float32),
        ] + [jax.ShapeDtypeStruct((2, rows, groups * HD), jnp.bfloat16)] * SPAN
    else:
        out_specs = [narrow, pair]
        out_shape = [
            jax.ShapeDtypeStruct((rows, heads // chunks * HD), jnp.bfloat16),
            jax.ShapeDtypeStruct(kv.shape, jnp.float32),
        ]
    return pl.pallas_call(
        functools.partial(backward_kernel, c, chunks, ratio),
        grid=(groups,),
        in_specs=[
            wide,
            pair,
            pl.BlockSpec((1, 1, per, window, rows), lambda g: (c, g, 0, 0, 0)),
            narrow,
            narrow,
        ]
        + ([narrow] * c + [pair] if c > 0 else []),
        out_specs=out_specs,
        out_shape=out_shape,
        cost_estimate=pl.CostEstimate(
            flops=16 * heads // chunks * rows * window * HD,
            bytes_accessed=2 * heads // chunks * rows * window,
            transcendentals=0,
        ),
    )(queries, kv, shares, d_attended, attended, *earlier)


def whole_step(queries, keys, values, output_grad, out_weight, lengths):
    block_rows = queries.shape[0]
    device = lax.axis_index("dp")
    side = lax.axis_index("head")
    two_sided = lax.axis_size("head") == 2
    own_width = output_grad.shape[1]
    depth = out_weight.shape[0]
    held = out_weight
    couple = jnp.stack([keys, values])
    earlier = [passed_along(couple, "dp", offset) for offset in range(1, SPAN + 1)]
    kv = jnp.concatenate(earlier[::-1] + [couple], axis=1)
    if two_sided:
        other = swapped(output_grad, "head")
        upstream_all = jnp.where(
            side == 0,
            jnp.concatenate([output_grad, other], axis=1),
            jnp.concatenate([other, output_grad], axis=1),
        )
    else:
        upstream_all = lax.all_gather(output_grad, "head", axis=1, tiled=True)

    positions = device * block_rows + jnp.arange(block_rows, dtype=jnp.int32)
    starts = doc_start(lengths, positions) - (device - SPAN) * block_rows
    attended, shares = attend_forward(starts[None, :], queries, kv, 1)

    if two_sided:
        chips = lax.axis_size("dp") // 2
        cycle = list(range(0, chips, 2)) + list(range(chips - 1, 0, -2))
        place_of = jnp.array([cycle.index(chip) for chip in range(chips)], jnp.int32)
        chip_at = jnp.array(cycle, jnp.int32)
        onward = []
        for r, chip in enumerate(cycle):
            onward.append((2 * chip, 2 * cycle[(r + 1) % chips]))
            onward.append((2 * chip + 1, 2 * cycle[(r - 1) % chips] + 1))
        partner = [(i, i ^ 1) for i in range(2 * chips)]
        place, core = place_of[device // 2], device % 2
        d_attended = jnp.zeros((block_rows, queries.shape[1]), jnp.bfloat16)
        projected = jnp.zeros((block_rows, upstream_all.shape[1]), jnp.float32)
        for step in range(chips):
            paired = lax.ppermute(held, "dp", partner)
            following = held
            if step < chips - 1:
                following = lax.ppermute(held, "dp", onward)
            up = 2 * chip_at[(place - step) % chips]
            down = 2 * chip_at[(place + step) % chips] + 1
            for block, owner in (
                (held, jnp.where(core == 0, up, down)),
                (paired, jnp.where(core == 0, down, up)),
            ):
                part = mm(upstream_all, block, (1, 1)).astype(jnp.bfloat16)
                d_attended = lax.dynamic_update_slice_in_dim(d_attended, part, owner * depth, 1)
                columns = lax.dynamic_slice_in_dim(attended, owner * depth, depth, 1)
                projected = projected + mm(columns, block, (1, 0))
            held = following
        theirs = lax.dynamic_slice_in_dim(projected, (1 - side) * own_width, own_width, 1)
        ours = lax.dynamic_slice_in_dim(projected, side * own_width, own_width, 1)
    else:
        weights = lax.all_gather(out_weight, "dp", axis=0, tiled=True)
        d_attended = mm(upstream_all, weights, (1, 1)).astype(jnp.bfloat16)
        ours = theirs = mm(attended, weights, (1, 0))
    d_attended, theirs = lax.optimization_barrier((d_attended, theirs.astype(jnp.bfloat16)))
    query_grad, *sums = attend_backward(
        0, 1, queries, kv, shares, d_attended, attended, []
    )

    if two_sided:
        arrived = swapped(theirs, "head")
        layer_out = (ours + arrived.astype(jnp.float32)).astype(jnp.bfloat16)
    else:
        layer_out = lax.psum_scatter(theirs, "head", scatter_dimension=1, tiled=True)
    home = sums[0]
    for offset in range(1, SPAN + 1):
        home = home + passed_along(sums[offset], "dp", -offset).astype(jnp.float32)
    home = home.astype(jnp.bfloat16)
    return layer_out, query_grad, home[0], home[1]


def solution(mesh):
    return jax.shard_map(
        whole_step,
        mesh=mesh,
        in_specs=(
            P("dp", "head"),
            P("dp", "head"),
            P("dp", "head"),
            P("dp", "head"),
            P(("head", "dp"), None),
            P(),
        ),
        out_specs=(P("dp", "head"), P("dp", "head"), P("dp", "head"), P("dp", "head")),
        check_vma=False,
    )
```

```python
import functools
import math

import jax
import jax.numpy as jnp
from jax import lax
from jax.experimental import pallas as pl
from jax.sharding import PartitionSpec as P

HD = 128
SPAN = 2

masked_score = -1e30


def passed_along(block, axis, distance):
    devices = range(lax.axis_size(axis))
    route = [(i - distance, i) for i in devices if i - distance in devices]
    return lax.ppermute(block, axis, route)


def swapped(block, axis):
    return lax.ppermute(block, axis, [(0, 1), (1, 0)])


def doc_start(lengths, positions):
    doc_ends = jnp.cumsum(lengths)
    closed = doc_ends[None, :] <= positions[:, None]
    return jnp.sum(jnp.where(closed, lengths[None, :], 0), axis=1)


def mm(a, b, contract):
    return lax.dot_general(a, b, ((contract[:1], contract[1:]), ((), ())), preferred_element_type=jnp.float32)


def forward_kernel(chunks, ratio, skipped, starts_ref, q_ref, kv_ref, *outs):
    outs = outs[skipped:]
    att_refs, shares_ref = outs[:chunks], outs[chunks]
    rows = q_ref.shape[0]
    window = kv_ref.shape[1]
    keys = kv_ref[0]
    values_t = kv_ref[1].T
    key_pos = lax.broadcasted_iota(jnp.int32, (window, rows), 0)
    query_pos = lax.broadcasted_iota(jnp.int32, (window, rows), 1) + (window - rows)
    visible = (key_pos >= starts_ref[...]) & (key_pos <= query_pos)
    scaling = 1.0 / math.sqrt(HD)
    for h in range(ratio):
        c, j = h % chunks, h // chunks
        scores = mm(keys, q_ref[:, h * HD : (h + 1) * HD], (1, 1)) * scaling
        scores = jnp.where(visible, scores, masked_score)
        weights = jnp.exp(scores - jnp.max(scores, axis=0, keepdims=True))
        shares = (weights * (1.0 / jnp.sum(weights, axis=0, keepdims=True))).astype(jnp.bfloat16)
        shares_ref[c, 0, j] = shares
        attended = mm(values_t, shares, (1, 0))
        att_refs[c][:, j * HD : (j + 1) * HD] = attended.T.astype(jnp.bfloat16)


def attend_forward(starts, queries, kv, chunks, part, parts, before=None):
    rows, heads = queries.shape[0], queries.shape[1] // HD
    window, groups = kv.shape[1], kv.shape[2] // HD
    ratio = heads // groups
    per = ratio // chunks
    span = groups // parts
    base = part * span
    extra = [] if before is None else [before]
    return pl.pallas_call(
        functools.partial(forward_kernel, chunks, ratio, len(extra)),
        grid=(span,),
        in_specs=[
            pl.BlockSpec((1, rows), lambda g: (0, 0)),
            pl.BlockSpec((rows, ratio * HD), lambda g: (0, g + base)),
            pl.BlockSpec((2, window, HD), lambda g: (0, 0, g + base)),
        ]
        + [pl.BlockSpec(memory_space=pl.ANY)] * len(extra),
        out_specs=[pl.BlockSpec((rows, per * HD), lambda g: (0, g + base))] * chunks
        + [pl.BlockSpec((chunks, 1, per, window, rows), lambda g: (0, g, 0, 0, 0))],
        out_shape=[jax.ShapeDtypeStruct((rows, heads // chunks * HD), jnp.bfloat16)] * chunks
        + [jax.ShapeDtypeStruct((chunks, span, per, window, rows), jnp.bfloat16)],
        input_output_aliases={3: 0} if extra else {},
        cost_estimate=pl.CostEstimate(
            flops=4 * heads // parts * rows * window * HD,
            bytes_accessed=2 * heads // parts * rows * window,
            transcendentals=heads // parts * rows * window,
        ),
    )(starts, queries, kv, *extra)


def backward_kernel(ratio, skipped, q_ref, kv_ref, shares_ref, da_ref, att_ref, *outs):
    dq_ref, home_ref, *away_refs = outs[skipped:]
    rows = q_ref.shape[0]
    window = kv_ref.shape[1]
    keys_t = kv_ref[0].T
    values = kv_ref[1]
    scaling = 1.0 / math.sqrt(HD)
    dk = jnp.zeros((window, HD), jnp.float32)
    dv = jnp.zeros((window, HD), jnp.float32)
    for h in range(ratio):
        da = da_ref[:, h * HD : (h + 1) * HD]
        att = att_ref[:, h * HD : (h + 1) * HD]
        shares = shares_ref[0, 0, h]
        row_dots = jnp.sum((da.astype(jnp.float32) * att.astype(jnp.float32)).T, axis=0, keepdims=True)
        d_shares = mm(values, da, (1, 1))
        dscore = (shares.astype(jnp.float32) * ((d_shares - row_dots) * scaling)).astype(jnp.bfloat16)
        dq_ref[:, h * HD : (h + 1) * HD] = mm(keys_t, dscore, (1, 0)).T.astype(jnp.bfloat16)
        dk = dk + mm(dscore, q_ref[:, h * HD : (h + 1) * HD], (1, 0))
        dv = dv + mm(shares, da, (1, 0))
    for part, total in ((0, dk), (1, dv)):
        home_ref[part] = total[window - rows :]
        for offset in range(1, SPAN + 1):
            first = window - (offset + 1) * rows
            away_refs[offset - 1][part] = total[first : first + rows].astype(jnp.bfloat16)


def attend_backward(queries, kv, shares, d_attended, attended, part, parts, before=None):
    rows, heads = queries.shape[0], queries.shape[1] // HD
    window, groups = kv.shape[1], kv.shape[2] // HD
    ratio = heads // groups
    span = groups // parts
    base = part * span
    extra = [] if before is None else [before]
    wide = pl.BlockSpec((rows, ratio * HD), lambda g: (0, g + base))
    home = pl.BlockSpec((2, rows, HD), lambda g: (0, 0, g))
    return pl.pallas_call(
        functools.partial(backward_kernel, ratio, len(extra)),
        grid=(span,),
        in_specs=[
            wide,
            pl.BlockSpec((2, window, HD), lambda g: (0, 0, g + base)),
            pl.BlockSpec((1, 1, ratio, window, rows), lambda g: (0, g, 0, 0, 0)),
            wide,
            wide,
        ]
        + [pl.BlockSpec(memory_space=pl.ANY)] * len(extra),
        out_specs=[wide] + [home] * (SPAN + 1),
        out_shape=[
            jax.ShapeDtypeStruct(queries.shape, jnp.bfloat16),
            jax.ShapeDtypeStruct((2, rows, span * HD), jnp.float32),
        ]
        + [jax.ShapeDtypeStruct((2, rows, span * HD), jnp.bfloat16)] * SPAN,
        input_output_aliases={5: 0} if extra else {},
        cost_estimate=pl.CostEstimate(
            flops=8 * heads // parts * rows * window * HD,
            bytes_accessed=2 * heads // parts * rows * window,
            transcendentals=0,
        ),
    )(queries, kv, shares, d_attended, attended, *extra)


def whole_step(queries, keys, values, output_grad, out_weight, lengths):
    block_rows = queries.shape[0]
    device = lax.axis_index("dp")
    side = lax.axis_index("head")
    two_sided = lax.axis_size("head") == 2
    own_width = output_grad.shape[1]
    depth = out_weight.shape[0]
    groups = keys.shape[1] // HD
    parts = 2 if groups % 2 == 0 else 1

    couple = jnp.stack([keys, values])
    earlier = []
    for offset in range(1, SPAN + 1):
        earlier.append(passed_along(couple, "dp", offset))
    kv = jnp.concatenate(earlier[::-1] + [couple], axis=1)
    if two_sided:
        other = swapped(output_grad, "head")
        upstream = (jnp.where(side == 0, output_grad, other), jnp.where(side == 0, other, output_grad))
    else:
        upstream_all = lax.all_gather(output_grad, "head", axis=1, tiled=True)

    positions = device * block_rows + jnp.arange(block_rows, dtype=jnp.int32)
    starts = doc_start(lengths, positions) - (device - SPAN) * block_rows
    attended, shares = None, []
    for part in range(parts):
        attended, share = attend_forward(
            starts[None, :], queries, kv, 1, part, parts, attended
        )
        shares.append(share)

    if two_sided:
        chips = lax.axis_size("dp") // 2
        cycle = list(range(0, chips, 2)) + list(range(chips - 1, 0, -2))
        half = len(range(0, chips, 2))

        def chip_at(spot):
            spot = jnp.where(spot < 0, spot + chips, jnp.where(spot >= chips, spot - chips, spot))
            return jnp.where(spot < half, 2 * spot, 2 * (chips - spot) - 1)

        onward = []
        for r, chip in enumerate(cycle):
            onward.append((2 * chip, 2 * cycle[(r + 1) % chips]))
            onward.append((2 * chip + 1, 2 * cycle[(r - 1) % chips] + 1))
        partner = [(i, i ^ 1) for i in range(2 * chips)]
        chip, core = device // 2, device % 2
        place = jnp.where(chip % 2 == 0, chip // 2, chips - 1 - chip // 2)
        held = [out_weight[:, :own_width], out_weight[:, own_width:]]
        d_attended = jnp.zeros((block_rows, queries.shape[1]), jnp.bfloat16)
        projected = [jnp.zeros((block_rows, own_width), jnp.float32)] * 2
        for step in range(chips):
            paired, following = [], list(held)
            for n in range(2):
                if step < chips - 1:
                    following[n] = lax.ppermute(held[n], "dp", onward)
                paired.append(lax.ppermute(held[n], "dp", partner))
            up = 2 * chip_at(place - step)
            down = 2 * chip_at(place + step) + 1
            for block, owner in (
                (held, jnp.where(core == 0, up, down)),
                (paired, jnp.where(core == 0, down, up)),
            ):
                part = (mm(upstream[0], block[0], (1, 1)) + mm(upstream[1], block[1], (1, 1))).astype(jnp.bfloat16)
                d_attended = lax.dynamic_update_slice_in_dim(d_attended, part, owner * depth, 1)
                columns = lax.dynamic_slice_in_dim(attended, owner * depth, depth, 1)
                projected = [projected[n] + mm(columns, block[n], (1, 0)) for n in range(2)]
            held = following
        theirs = jnp.where(side == 0, projected[1], projected[0])
        ours = jnp.where(side == 0, projected[0], projected[1])
    else:
        weights = lax.all_gather(out_weight, "dp", axis=0, tiled=True)
        d_attended = mm(upstream_all, weights, (1, 1)).astype(jnp.bfloat16)
        ours = theirs = mm(attended, weights, (1, 0))
    d_attended, theirs = lax.optimization_barrier((d_attended, theirs.astype(jnp.bfloat16)))
    query_grad, homes = None, []
    for part in range(parts):
        query_grad, home, *sums = attend_backward(
            queries, kv, shares[part], d_attended, attended, part, parts, query_grad
        )
        for offset in range(1, SPAN + 1):
            home = home + passed_along(sums[offset - 1], "dp", -offset).astype(jnp.float32)
        homes.append(home.astype(jnp.bfloat16))

    if two_sided:
        arrived = swapped(theirs, "head")
        layer_out = (ours + arrived.astype(jnp.float32)).astype(jnp.bfloat16)
    else:
        layer_out = lax.psum_scatter(theirs, "head", scatter_dimension=1, tiled=True)
    key_grad = jnp.concatenate([home[0] for home in homes], axis=1)
    value_grad = jnp.concatenate([home[1] for home in homes], axis=1)
    return layer_out, query_grad, key_grad, value_grad


def solution(mesh):
    return jax.shard_map(
        whole_step,
        mesh=mesh,
        in_specs=(
            P("dp", "head"),
            P("dp", "head"),
            P("dp", "head"),
            P("dp", "head"),
            P(("head", "dp"), None),
            P(),
        ),
        out_specs=(P("dp", "head"), P("dp", "head"), P("dp", "head"), P("dp", "head")),
        check_vma=False,
    )
```

```python
import functools
import math

import jax
import jax.numpy as jnp
from jax import lax
from jax.experimental import pallas as pl
from jax.experimental.pallas import tpu as pltpu
from jax.sharding import PartitionSpec as P

HD = 128
SPAN = 2
PAIR = 2

masked_score = -1e30


def passed_along(block, axis, distance):
    devices = range(lax.axis_size(axis))
    route = [(i - distance, i) for i in devices if i - distance in devices]
    return lax.ppermute(block, axis, route)


def swapped(block, axis):
    return lax.ppermute(block, axis, [(0, 1), (1, 0)])


def doc_start(lengths, positions):
    doc_ends = jnp.cumsum(lengths)
    closed = doc_ends[None, :] <= positions[:, None]
    return jnp.sum(jnp.where(closed, lengths[None, :], 0), axis=1)


def mm(a, b, contract):
    return lax.dot_general(a, b, ((contract[:1], contract[1:]), ((), ())), preferred_element_type=jnp.float32)


def forward_kernel(chunks, ratio, skipped, starts_ref, q_ref, kv_ref, *outs):
    outs = outs[skipped:]
    att_refs, shares_ref = outs[:chunks], outs[chunks]
    rows = q_ref.shape[0]
    window = kv_ref.shape[1]
    keys = kv_ref[0]
    values_t = kv_ref[1].T
    key_pos = lax.broadcasted_iota(jnp.int32, (window, rows), 0)
    query_pos = lax.broadcasted_iota(jnp.int32, (window, rows), 1) + (window - rows)
    visible = (key_pos >= starts_ref[...]) & (key_pos <= query_pos)
    scaling = 1.0 / math.sqrt(HD)

    def heads(pair, carry):
        for _ in range(1):
            h = pair
            columns = pl.ds(pl.multiple_of(h * HD, HD), HD)
            scores = mm(keys, q_ref[:, columns], (1, 1)) * scaling
            scores = jnp.where(visible, scores, masked_score)
            weights = jnp.exp(scores - jnp.max(scores, axis=0, keepdims=True))
            shares = (weights * (1.0 / jnp.sum(weights, axis=0, keepdims=True))).astype(jnp.bfloat16)
            shares_ref[0, 0, h] = shares
            att_refs[0][:, columns] = mm(values_t, shares, (1, 0)).T.astype(jnp.bfloat16)
        return carry

    lax.fori_loop(0, ratio, heads, 0)


def attend_forward(starts, queries, kv, chunks, part, parts, before=None):
    rows, heads = queries.shape[0], queries.shape[1] // HD
    window, groups = kv.shape[1], kv.shape[2] // HD
    ratio = heads // groups
    per = ratio // chunks
    span = groups // parts
    base = part * span
    extra = [] if before is None else [before]
    return pl.pallas_call(
        functools.partial(forward_kernel, chunks, ratio, len(extra)),
        grid=(span,),
        in_specs=[
            pl.BlockSpec((1, rows), lambda g: (0, 0)),
            pl.BlockSpec((rows, ratio * HD), lambda g: (0, g + base)),
            pl.BlockSpec((2, window, HD), lambda g: (0, 0, g + base)),
        ]
        + [pl.BlockSpec(memory_space=pl.ANY)] * len(extra),
        out_specs=[pl.BlockSpec((rows, per * HD), lambda g: (0, g + base))] * chunks
        + [pl.BlockSpec((chunks, 1, per, window, rows), lambda g: (0, g, 0, 0, 0))],
        out_shape=[jax.ShapeDtypeStruct((rows, heads // chunks * HD), jnp.bfloat16)] * chunks
        + [jax.ShapeDtypeStruct((chunks, span, per, window, rows), jnp.bfloat16)],
        input_output_aliases={3: 0} if extra else {},
        cost_estimate=pl.CostEstimate(
            flops=4 * heads // parts * rows * window * HD,
            bytes_accessed=2 * heads // parts * rows * window,
            transcendentals=heads // parts * rows * window,
        ),
    )(starts, queries, kv, *extra)


def backward_kernel(ratio, skipped, q_ref, kv_ref, shares_ref, da_ref, att_ref, *outs):
    dq_ref, home_ref, *away_refs, dk_ref, dv_ref = outs[skipped:]
    rows = q_ref.shape[0]
    window = kv_ref.shape[1]
    keys_t = kv_ref[0].T
    values = kv_ref[1]
    scaling = 1.0 / math.sqrt(HD)
    dk_ref[...] = jnp.zeros((window, HD), jnp.float32)
    dv_ref[...] = jnp.zeros((window, HD), jnp.float32)

    def heads(pair, carry):
        dk, dv = dk_ref[...], dv_ref[...]
        for side in range(PAIR):
            h = pair * PAIR + side
            columns = pl.ds(pl.multiple_of(h * HD, HD), HD)
            da = da_ref[:, columns]
            shares = shares_ref[0, 0, h]
            product = da.astype(jnp.float32) * att_ref[:, columns].astype(jnp.float32)
            row_dots = jnp.sum(product.T, axis=0, keepdims=True)
            d_shares = mm(values, da, (1, 1))
            dscore = (shares.astype(jnp.float32) * ((d_shares - row_dots) * scaling)).astype(jnp.bfloat16)
            dq_ref[:, columns] = mm(keys_t, dscore, (1, 0)).T.astype(jnp.bfloat16)
            dk = dk + mm(dscore, q_ref[:, columns], (1, 0))
            dv = dv + mm(shares, da, (1, 0))
        dk_ref[...] = dk
        dv_ref[...] = dv
        return carry

    lax.fori_loop(0, ratio // PAIR, heads, 0)
    dk, dv = dk_ref[...], dv_ref[...]
    for part, total in ((0, dk), (1, dv)):
        home_ref[part] = total[window - rows :]
        for offset in range(1, SPAN + 1):
            first = window - (offset + 1) * rows
            away_refs[offset - 1][part] = total[first : first + rows].astype(jnp.bfloat16)


def attend_backward(queries, kv, shares, d_attended, attended, part, parts, before=None):
    rows, heads = queries.shape[0], queries.shape[1] // HD
    window, groups = kv.shape[1], kv.shape[2] // HD
    ratio = heads // groups
    span = groups // parts
    base = part * span
    extra = [] if before is None else [before]
    wide = pl.BlockSpec((rows, ratio * HD), lambda g: (0, g + base))
    home = pl.BlockSpec((2, rows, HD), lambda g: (0, 0, g))
    return pl.pallas_call(
        functools.partial(backward_kernel, ratio, len(extra)),
        grid=(span,),
        in_specs=[
            wide,
            pl.BlockSpec((2, window, HD), lambda g: (0, 0, g + base)),
            pl.BlockSpec((1, 1, ratio, window, rows), lambda g: (0, g, 0, 0, 0)),
            wide,
            wide,
        ]
        + [pl.BlockSpec(memory_space=pl.ANY)] * len(extra),
        out_specs=[wide] + [home] * (SPAN + 1),
        out_shape=[
            jax.ShapeDtypeStruct(queries.shape, jnp.bfloat16),
            jax.ShapeDtypeStruct((2, rows, span * HD), jnp.float32),
        ]
        + [jax.ShapeDtypeStruct((2, rows, span * HD), jnp.bfloat16)] * SPAN,
        scratch_shapes=[pltpu.VMEM((window, HD), jnp.float32)] * 2,
        input_output_aliases={5: 0} if extra else {},
        cost_estimate=pl.CostEstimate(
            flops=8 * heads // parts * rows * window * HD,
            bytes_accessed=2 * heads // parts * rows * window,
            transcendentals=0,
        ),
    )(queries, kv, shares, d_attended, attended, *extra)


def whole_step(queries, keys, values, output_grad, out_weight, lengths):
    block_rows = queries.shape[0]
    device = lax.axis_index("dp")
    side = lax.axis_index("head")
    two_sided = lax.axis_size("head") == 2
    own_width = output_grad.shape[1]
    depth = out_weight.shape[0]
    groups = keys.shape[1] // HD
    parts = 2 if groups % 2 == 0 else 1

    couple = jnp.stack([keys, values])
    earlier = []
    for offset in range(1, SPAN + 1):
        earlier.append(passed_along(couple, "dp", offset))
    kv = jnp.concatenate(earlier[::-1] + [couple], axis=1)
    if two_sided:
        other = swapped(output_grad, "head")
        upstream = (jnp.where(side == 0, output_grad, other), jnp.where(side == 0, other, output_grad))
    else:
        upstream_all = lax.all_gather(output_grad, "head", axis=1, tiled=True)

    positions = device * block_rows + jnp.arange(block_rows, dtype=jnp.int32)
    starts = doc_start(lengths, positions) - (device - SPAN) * block_rows
    attended, shares = None, []
    for part in range(parts):
        attended, share = attend_forward(
            starts[None, :], queries, kv, 1, part, parts, attended
        )
        shares.append(share)

    if two_sided:
        chips = lax.axis_size("dp") // 2
        cycle = list(range(0, chips, 2)) + list(range(chips - 1, 0, -2))
        half = len(range(0, chips, 2))

        def chip_at(spot):
            spot = jnp.where(spot < 0, spot + chips, jnp.where(spot >= chips, spot - chips, spot))
            return jnp.where(spot < half, 2 * spot, 2 * (chips - spot) - 1)

        onward = []
        for r, chip in enumerate(cycle):
            onward.append((2 * chip, 2 * cycle[(r + 1) % chips]))
            onward.append((2 * chip + 1, 2 * cycle[(r - 1) % chips] + 1))
        partner = [(i, i ^ 1) for i in range(2 * chips)]
        chip, core = device // 2, device % 2
        place = jnp.where(chip % 2 == 0, chip // 2, chips - 1 - chip // 2)
        held = [out_weight[:, :own_width], out_weight[:, own_width:]]
        d_attended = jnp.zeros((block_rows, queries.shape[1]), jnp.bfloat16)
        projected = [jnp.zeros((block_rows, own_width), jnp.float32)] * 2
        for step in range(chips):
            paired, following = [], list(held)
            for n in range(2):
                if step < chips - 1:
                    following[n] = lax.ppermute(held[n], "dp", onward)
                paired.append(lax.ppermute(held[n], "dp", partner))
            up = 2 * chip_at(place - step)
            down = 2 * chip_at(place + step) + 1
            for block, owner in (
                (held, jnp.where(core == 0, up, down)),
                (paired, jnp.where(core == 0, down, up)),
            ):
                part = (mm(upstream[0], block[0], (1, 1)) + mm(upstream[1], block[1], (1, 1))).astype(jnp.bfloat16)
                d_attended = lax.dynamic_update_slice_in_dim(d_attended, part, owner * depth, 1)
                columns = lax.dynamic_slice_in_dim(attended, owner * depth, depth, 1)
                projected = [projected[n] + mm(columns, block[n], (1, 0)) for n in range(2)]
            held = following
        theirs = jnp.where(side == 0, projected[1], projected[0])
        ours = jnp.where(side == 0, projected[0], projected[1])
    else:
        weights = lax.all_gather(out_weight, "dp", axis=0, tiled=True)
        d_attended = mm(upstream_all, weights, (1, 1)).astype(jnp.bfloat16)
        ours = theirs = mm(attended, weights, (1, 0))
    d_attended, theirs = lax.optimization_barrier((d_attended, theirs.astype(jnp.bfloat16)))
    query_grad, homes = None, []
    for part in range(parts):
        query_grad, home, *sums = attend_backward(
            queries, kv, shares[part], d_attended, attended, part, parts, query_grad
        )
        for offset in range(1, SPAN + 1):
            home = home + passed_along(sums[offset - 1], "dp", -offset).astype(jnp.float32)
        homes.append(home.astype(jnp.bfloat16))

    if two_sided:
        arrived = swapped(theirs, "head")
        layer_out = (ours + arrived.astype(jnp.float32)).astype(jnp.bfloat16)
    else:
        layer_out = lax.psum_scatter(theirs, "head", scatter_dimension=1, tiled=True)
    key_grad = jnp.concatenate([home[0] for home in homes], axis=1)
    value_grad = jnp.concatenate([home[1] for home in homes], axis=1)
    return layer_out, query_grad, key_grad, value_grad


def solution(mesh):
    return jax.shard_map(
        whole_step,
        mesh=mesh,
        in_specs=(
            P("dp", "head"),
            P("dp", "head"),
            P("dp", "head"),
            P("dp", "head"),
            P(("head", "dp"), None),
            P(),
        ),
        out_specs=(P("dp", "head"), P("dp", "head"), P("dp", "head"), P("dp", "head")),
        check_vma=False,
    )
```
